512 devices in a mesh: section: 16 (over z_lo, x), seq: 32 (over z_hi, y, core).
Axes of the slice: x: 4, y: 8, z: 8 (z_hi: 2, z_lo: 4; z = z_hi * 4 + z_lo), core: 2. Of those that a mesh axis runs over, the one named last changes fastest.
Arguments:
- features: bfloat16 [16, 4096, 4096], P('section', 'seq'), may hold values from -6 to 6
- queries: bfloat16 [16, 4096, 4096], P('section', 'seq'), may hold values from -52 to 52
- out_grad: bfloat16 [16, 4096, 4096], P('section', 'seq'), may hold values from -0.09375 to 0.09375
- doc_ids: int32 [16, 4096], P('section', 'seq'), may hold values from 0 to 15, never falling along the last dimension, each value on 1 to 512 neighbouring positions
- key_weight: bfloat16 [4096, 512], P('section'), may hold values from -0.09375 to 0.09375
Outputs:
- value_weight_grad: float32 [4096, 512], P('seq', 'section')
The draws below stay inside these ranges and needn't reach their ends.
All inputs are finite; a program needn't handle non-finite values.
Results may differ from the reference program's by a relative error of at most 0.012.
Values may be sent and summed in bfloat16 or wider, within the bound.
No kernel may reach another device: no remote copies, remote signals or barrier semaphores. Data moves between devices by JAX's collectives and lax.ppermute only.
A program may use at most 64 MiB of HBM per device.

```python
import math
import jax
import jax.numpy as jnp
import numpy as np
from jax import lax

D = 4096
HQ = 32
KVH = 4
HD = 128
TOK_DEV = 128
REACH = 4
MOST = 512
LEN = 4096
MB = 16
N_SECTION = 16
N_SEQ = 32


def draw_queries(key, part):
    shape_full = (MB, LEN, HQ * HD)
    values = jnp.clip(jax.random.normal(key, shape_full, jnp.float32), -6.0, 6.0)
    return values.astype(jnp.bfloat16)


def block_levels(key, dims, shards, low, largest):
    def one(position, shards_of):
        heights = jax.random.uniform(jax.random.fold_in(jax.random.fold_in(key, 6), position), (shards_of,), jnp.float32, low / len(shards), largest / len(shards))
        return jnp.repeat(jnp.exp(heights), dims[position] // shards_of).reshape((-1,) + (1,) * (len(dims) - position - 1))

    loudness = one(*shards[0])
    for cut in shards[1:]:
        loudness = loudness * one(*cut)
    return loudness


def split_up(count, total, most, slope):
    loads = [(1 << 20) // math.isqrt(rank ** slope) + 1 for rank in range(2, count + 1)]
    surplus, counts = total - most - (count - 1), [1] * (count - 1)
    while surplus > 0:
        candidates = [i for i in range(count - 1) if counts[i] < most]
        mass, left = sum([loads[i] for i in candidates]), surplus
        for i in candidates:
            addition = min(most - counts[i], max(1, left * loads[i] // mass), surplus)
            counts[i] = counts[i] + addition
            surplus = surplus - addition
    return np.array([most] + counts)


def ragged_sizes(key, amount, total, reach, slope):
    if amount == 2:
        one = jax.random.randint(key, (), max(1, total - reach), min(reach, total - 1) + 1)
        return jnp.stack([one, total - one])
    sizes = jnp.asarray(split_up(amount, total, reach, slope), jnp.int32)
    twos = (amount - 1) // 2
    giver, receiver = sizes[1:1 + 2 * twos:2], sizes[2:2 + 2 * twos:2]
    room = jnp.minimum(giver - 1, reach - receiver)
    moved = jax.random.randint(jax.random.fold_in(key, 1), (twos,), 0, 1 << 20) % (room + 1)
    sizes = sizes.at[1:1 + 2 * twos:2].set(giver - moved).at[2:2 + 2 * twos:2].set(receiver + moved)
    return sizes[jax.random.permutation(jax.random.fold_in(key, 2), amount)]


def centred(stream_key, dims, scale, most, shards=(), kind=jnp.bfloat16):
    loudness = block_levels(stream_key, dims, shards, -0.22, 0.18) if shards else 1.0
    values = jax.random.normal(stream_key, dims, jnp.float32) * scale * loudness
    return jnp.minimum(jnp.maximum(values, -most), most).astype(kind)


def setup_inputs(seed: int = 0) -> dict:
    key_list = jax.random.split(jax.random.key(seed), 6)
    features = centred(key_list[0], (MB, LEN, D), 1.0, 6.0, ((0, 16), (1, 32)))
    queries = draw_queries(jax.random.fold_in(key_list[5], 71), 0)
    out_grad = centred(key_list[2], (MB, LEN, HQ * HD), (4.0 / (TOK_DEV * N_SEQ * N_SECTION) ** 0.5), 0.09375, ((0, 16), (1, 32)))
    doc_ids = jax.vmap(lambda own: jnp.searchsorted(jnp.cumsum(ragged_sizes(own, 2 * N_SEQ // REACH, LEN, MOST, 2)), jnp.arange(LEN), side="right"))(jax.random.split(key_list[3], MB)).reshape((MB, LEN)).astype(jnp.int32)
    key_weight = centred(key_list[4], (D, KVH * HD), D ** -0.5, 0.09375, ((0, 16),))
    return {"features": features, "queries": queries, "out_grad": out_grad, "doc_ids": doc_ids, "key_weight": key_weight}


def reference(features, queries, out_grad, doc_ids, key_weight):
    kv_width = KVH * HD
    group_size = HQ // KVH
    margin = REACH * TOK_DEV
    window_len = margin + TOK_DEV
    score_scale = 1.0 / math.sqrt(HD)

    def one_batch(running, items):
        feat_rows, query_all, grad_all, doc_all = items
        keys_all = jnp.dot(feat_rows, key_weight, preferred_element_type=jnp.float32).astype(jnp.bfloat16)
        keys_pad = jnp.concatenate([jnp.zeros((margin, kv_width), keys_all.dtype), keys_all], axis=0)
        docs_pad = jnp.concatenate([jnp.full((margin,), -1, jnp.int32), doc_all.astype(jnp.int32)], axis=0)

        def block(index):
            first_row = (index * TOK_DEV).astype(jnp.int32)
            key_win = lax.dynamic_slice_in_dim(keys_pad, first_row, window_len, 0)
            doc_win = lax.dynamic_slice_in_dim(docs_pad, first_row, window_len, 0)
            query_blk = lax.dynamic_slice_in_dim(query_all, first_row, TOK_DEV, 0)
            grad_blk = lax.dynamic_slice_in_dim(grad_all, first_row, TOK_DEV, 0)
            doc_blk = lax.dynamic_slice_in_dim(doc_all.astype(jnp.int32), first_row, TOK_DEV, 0)
            query_f = query_blk.astype(jnp.float32).reshape(TOK_DEV, KVH, group_size, HD)
            grad_f = grad_blk.astype(jnp.float32).reshape(TOK_DEV, KVH, group_size, HD)
            key_f = key_win.astype(jnp.float32).reshape(window_len, KVH, HD)
            scores = jnp.einsum('tgrd,wgd->tgrw', query_f, key_f) * score_scale
            query_pos = first_row + jnp.arange(TOK_DEV, dtype=jnp.int32)
            key_pos = first_row - margin + jnp.arange(window_len, dtype=jnp.int32)
            visible = (doc_blk[:, None] == doc_win[None, :]) & (key_pos[None, :] <= query_pos[:, None])
            mask_full = visible[:, None, None, :]
            masked = jnp.where(mask_full, scores, -1e+30)
            row_top = lax.optimization_barrier(jnp.max(masked, axis=3, keepdims=True))
            weights_exp = jnp.where(mask_full, jnp.exp(masked - row_top), 0.0)
            prob_rows = (weights_exp / lax.optimization_barrier(jnp.sum(weights_exp, axis=3, keepdims=True))).astype(jnp.bfloat16)
            window_grad = jnp.einsum('tgrw,tgrd->wgd', prob_rows.astype(jnp.float32), grad_f)
            return window_grad.reshape(REACH + 1, TOK_DEV, kv_width)
        pieces = lax.map(block, jnp.arange(N_SEQ, dtype=jnp.int32))
        padded = jnp.concatenate([pieces, jnp.zeros((REACH, REACH + 1, TOK_DEV, kv_width), pieces.dtype)], axis=0)
        summed = jnp.zeros((N_SEQ, TOK_DEV, kv_width), pieces.dtype)
        for hop_count in range(REACH + 1):
            summed = summed + padded[hop_count:hop_count + N_SEQ, REACH - hop_count]
        value_grad = summed.reshape(N_SEQ * TOK_DEV, kv_width).astype(jnp.bfloat16)
        contrib = jnp.dot(feat_rows.T, value_grad, preferred_element_type=jnp.float32)
        return (running + contrib, None)
    start_value = jnp.zeros((D, kv_width), jnp.float32)
    result, unused = lax.scan(one_batch, start_value, (features, queries, out_grad, doc_ids))
    return result
```

```python
import functools
import math

import jax
import jax.numpy as jnp
from jax import lax
from jax.experimental import pallas as pl
from jax.experimental.pallas import tpu as pltpu
from jax.sharding import Mesh
from jax.sharding import PartitionSpec as P

HQ = 32
KVH = 4
HD = 128
GROUP = HQ // KVH
REACH = 4
ZL, X, ZH, YQ, YB, C = "zl", "x", "zh", "yq", "yb", "core"
SECTION = (ZL, X)
SEQ = (ZH, YQ, YB, C)
CHIPS = (ZH, YQ, YB)
FAR = -1e30


def cyclic(x, axis, by):
    peers = lax.axis_size(axis)
    return lax.ppermute(x, axis, [(i, (i + by) % peers) for i in range(peers)])


def shifted(x, axis, by):
    peers = lax.axis_size(axis)
    pairs = [(i, i + by) for i in range(peers) if 0 <= i + by < peers]
    return lax.ppermute(x, axis, pairs)


def pick(index, halves):
    return jnp.where(index == 0, halves[0], halves[1])


def attention_kernel(tok, bias_ref, k_refs, q_refs, g_refs, far_ref, near_ref, own_ref):
    heads = k_refs[0].shape[1] // HD
    rate = math.log2(math.e) / math.sqrt(HD)
    bias = bias_ref
    for g in range(heads):
        cols = slice(g * HD, (g + 1) * HD)
        keys = jnp.concatenate([k[:, cols] for k in k_refs], axis=0)
        total = None
        for r in range(GROUP):
            h = g * GROUP + r
            wide = slice(h * HD, (h + 1) * HD)
            q = jnp.concatenate([x[:, wide] for x in q_refs], axis=0)
            grad = jnp.concatenate([x[:, wide] for x in g_refs], axis=0)
            scores = lax.dot_general(
                keys, q, (((1,), (1,)), ((), ())), preferred_element_type=jnp.float32
            )
            scores = scores + bias[...]
            top = jnp.max(scores, axis=0, keepdims=True)
            weight = jnp.exp2((scores - top) * rate)
            inverse = 1.0 / jnp.sum(weight, axis=0, keepdims=True)
            probs = (weight * inverse).astype(jnp.bfloat16)
            term = jnp.dot(probs, grad, preferred_element_type=jnp.float32)
            total = term if total is None else total + term
        far_ref[:, cols] = total[: 2 * tok].astype(far_ref.dtype)
        near_ref[:, cols] = total[2 * tok : 4 * tok].astype(near_ref.dtype)
        own_ref[:, cols] = total[4 * tok :]


def attention(bias, keys, queries, grads):
    tok, width = keys[-1].shape[0], keys[-1].shape[1]

    def kernel(*refs):
        n_k, n_q = len(keys), len(queries)
        bias_ref, refs = refs[0], refs[1:]
        k_refs, refs = refs[:n_k], refs[n_k:]
        q_refs, refs = refs[:n_q], refs[n_q:]
        g_refs, refs = refs[:n_q], refs[n_q:]
        attention_kernel(tok, bias_ref, k_refs, q_refs, g_refs, *refs)

    return pl.pallas_call(
        kernel,
        name="attention",
        out_shape=(
            jax.ShapeDtypeStruct((2 * tok, width), jnp.bfloat16),
            jax.ShapeDtypeStruct((2 * tok, width), jnp.bfloat16),
            jax.ShapeDtypeStruct((2 * tok, width), jnp.float32),
        ),
    )(bias, *keys, *queries, *grads)


def on_device(features, queries, out_grad, doc_ids, key_weight):
    tokens = features[0]
    tok, depth = tokens.shape
    core, x_at = lax.axis_index(C), lax.axis_index(X)
    n_zl, n_x = lax.axis_size(ZL), lax.axis_size(X)
    n_zh, n_yq = lax.axis_size(ZH), lax.axis_size(YQ)
    rows, kv_width = key_weight.shape
    half = kv_width // 2

    by_x = tokens.reshape(tok, n_zl, n_x, rows)

    def block_for(k):
        at = (x_at + k) % n_x
        return lax.dynamic_slice_in_dim(by_x, at, 1, 2).reshape(tok, n_zl * rows)

    parts = [block_for(0)] + [cyclic(block_for(k), X, k) for k in range(1, n_x)]

    mine = pick(core, (key_weight[:, :half], key_weight[:, half:]))
    weight_own = lax.all_gather(mine, ZL, tiled=True)
    weight_oth = cyclic(weight_own, C, 1)

    def partial(part):
        own = jnp.dot(part, weight_own, preferred_element_type=jnp.float32)
        oth = jnp.dot(part, weight_oth, preferred_element_type=jnp.float32)
        return jnp.concatenate([own, oth], axis=1)

    total = partial(parts[0])
    for k in range(1, n_x):
        total = total + cyclic(partial(parts[k]).astype(jnp.bfloat16), X, -k)
    keys = total.astype(jnp.bfloat16)
    keys_chip = jnp.concatenate([keys[:, :half], cyclic(keys[:, half:], C, 1)], axis=0)
    keys_near = shifted(keys_chip, CHIPS, 1)
    keys_far = shifted(keys_chip, CHIPS, 2)

    def both_cores(rows_all):
        wide = rows_all.shape[1] // 2
        first, last = rows_all[:, :wide], rows_all[:, wide:]
        return pick(core, (first, last)), cyclic(pick(core, (last, first)), C, 1)

    q_pair = both_cores(queries[0])
    g_pair = both_cores(out_grad[0])

    docs = doc_ids[0]
    docs_chip = jnp.concatenate([docs, cyclic(docs, C, 1)])
    docs_win = jnp.concatenate(
        [shifted(docs_chip, CHIPS, 2), shifted(docs_chip, CHIPS, 1), docs_chip]
    )
    chip = lax.axis_index(CHIPS)
    step = jnp.arange(tok, dtype=jnp.int32)
    pos_chip = jnp.concatenate([core * tok + step, (1 - core) * tok + step]) + chip * 2 * tok
    pos_win = jnp.concatenate([pos_chip - 4 * tok, pos_chip - 2 * tok, pos_chip])
    visible = (
        (docs_win[:, None] == docs_chip[None, :])
        & (pos_win[:, None] <= pos_chip[None, :])
        & (pos_win[:, None] >= 0)
    )
    bias = jnp.where(visible, 0.0, FAR).astype(jnp.float32)

    far, near, own = attention(bias, (keys_far, keys_near, keys_chip[:tok], keys_chip[tok:]), q_pair, g_pair)
    own = own + shifted(near, CHIPS, -1) + shifted(far, CHIPS, -2)
    value_chip = own.astype(jnp.bfloat16)
    value_all = jnp.concatenate([value_chip, cyclic(value_chip, YB, 1)], axis=0)

    yb_at = lax.axis_index(YB)
    by_yb = tokens.reshape(tok, n_zh * n_yq, 2, depth // (n_zh * n_yq * 2))
    first = by_yb[:, :, 0].reshape(tok, depth // 2)
    last = by_yb[:, :, 1].reshape(tok, depth // 2)
    own_rows = pick(yb_at, (first, last))
    pair_rows = cyclic(pick(yb_at, (last, first)), YB, 1)
    two = jnp.concatenate([own_rows, pair_rows], axis=0)
    four = cyclic(two, C, 1)
    feat_all = jnp.concatenate([two[:tok], four[:tok], two[tok:], four[tok:]], axis=0)

    block = lax.dot_general(
        value_all, feat_all, (((0,), (0,)), ((), ())), preferred_element_type=jnp.float32
    ).astype(jnp.bfloat16)
    n_zb = n_zl // 2
    out_cols = half // (n_zb * n_x)
    block = block.reshape(n_zb, n_x, out_cols, depth // 2).transpose(1, 0, 2, 3)
    arrived = lax.all_to_all(block, X, split_axis=0, concat_axis=0, tiled=True)
    summed = sum(arrived[k].astype(jnp.float32) for k in range(n_x)).astype(jnp.bfloat16)
    by_core = summed.reshape(n_zb, out_cols, n_zh * n_yq, 2, tok)
    keep = pick(core, (by_core[:, :, :, 0], by_core[:, :, :, 1]))
    give = pick(core, (by_core[:, :, :, 1], by_core[:, :, :, 0]))
    came = cyclic(give, C, 1)
    low, high = pick(core, (keep, came)), pick(core, (came, keep))
    last = jnp.concatenate([low, high], axis=0).transpose(0, 2, 1, 3)
    last = last.reshape(n_zl * n_zh * n_yq, out_cols, tok)
    ended = lax.all_to_all(last, (ZL, ZH, YQ), split_axis=0, concat_axis=0, tiled=True)
    return ended.astype(jnp.float32).sum(axis=0).T


def solution(mesh):
    n_section, n_seq = mesh.devices.shape
    sizes = (n_section // 4, 4, 2, n_seq // 8, 2, 2)
    finer = Mesh(mesh.devices.reshape(sizes), (ZL, X, ZH, YQ, YB, C))
    return jax.shard_map(
        on_device,
        mesh=finer,
        in_specs=(
            P(SECTION, SEQ, None),
            P(SECTION, SEQ, None),
            P(SECTION, SEQ, None),
            P(SECTION, SEQ),
            P(SECTION, None),
        ),
        out_specs=P(SEQ, SECTION),
        check_vma=False,
    )
```
